32 devices in a mesh: pb: 8 (over y, x, core), ga: 4 (over z).
Axes of the slice: x: 2, y: 2, z: 4, core: 2. Of those that a mesh axis runs over, the one named last changes fastest.
Arguments:
- query_points: float32 [3, 32768], P(None, 'pb'), may hold values from 0 to 1
- cotangent: bfloat16 [64, 32768], P(None, 'pb'), may hold values from -6 to 6
- slab_ids: int32 [8, 32768], P(None, 'pb'), may hold values from -1 to 3
- rel_cells: int32 [8, 32768], P(None, 'pb'), may hold values from 0 to 511
- offsets: int32 [4, 256], P('ga', 'pb'), may hold values from 0 to 15872
- latent: bfloat16 [4, 64, 16384], P('ga', None, 'pb'), may hold values from -6 to 6
- w_in: float32 [80, 6], replicated, may hold values from -2.5 to 2.5
- b_in: float32 [80], replicated, may hold values from -3 to 3
- w_out: bfloat16 [64, 80], replicated, may hold values from -0.625 to 0.625
- b_out: float32 [64], replicated, may hold values from -3 to 3
Outputs:
- grid_grad: float32 [4, 64, 16384], P('ga', None, 'pb')
- w_in_grad: float32 [80, 6], replicated
- b_in_grad: float32 [80], replicated
- w_out_grad: float32 [64, 80], replicated
- b_out_grad: float32 [64], replicated
The draws below stay inside these ranges and needn't reach their ends.
Inputs may be any that keep to these rules, and one draw needn't show every extreme that they name: `slab_ids`: -1 marks a padding slot; otherwise the slab that holds the neighbour cell.
All inputs are finite; a program needn't handle non-finite values.
Results may differ from the reference program's by a relative error of at most 0.0085.
Values may be sent and summed in bfloat16 or wider, within the bound.
No kernel may reach another device: no remote copies, remote signals or barrier semaphores. Data moves between devices by JAX's collectives and lax.ppermute only.
A program may use at most 64 MiB of HBM per device.

```python
import math
import jax
import jax.numpy as jnp
from jax import lax

CH = 64
HID = 80
KN = 8
TILE = 128
WIN = 512
GX = 64
ZS = 4
SLAB_CELLS = 16384
QUERIES = 32768
TILES = 256
N_GA = 4


def with_ends(array, rng, low, high):
    extent = array.shape
    spot = [jax.random.randint(jax.random.fold_in(rng, axis), (), 0, extent[axis]) for axis in range(len(extent))]
    array = array.at[tuple(spot)].set(low)
    longest = extent.index(max(extent))
    spot[longest] = (spot[longest] + 1) % extent[longest]
    return array.at[tuple(spot)].set(high)


def block_levels(rng, extent, split, least, top_value):
    loudness = 1.0
    for dim, blocks in split:
        draws = jax.random.uniform(jax.random.fold_in(jax.random.fold_in(rng, 6), dim), (blocks,), jnp.float32, least / len(split), top_value / len(split))
        loudness = loudness * jnp.repeat(jnp.exp(draws), extent[dim] // blocks).reshape((-1,) + (1,) * (len(extent) - 1 - dim))
    return loudness


def gaussian(rng, shape, deviation, bound, cuts=(), kind=jnp.bfloat16):
    drawn = jax.random.normal(rng, shape, jnp.float32) * deviation
    if len(cuts) > 0:
        drawn = block_levels(rng, shape, cuts, -0.22, 0.18) * drawn
    return jnp.clip(drawn, min=-bound, max=bound).astype(kind)


def setup_inputs(seed: int = 0) -> dict:
    key_list = jax.random.split(jax.random.key(seed), 11)
    return {
        "query_points": jnp.clip(1.0 * jax.random.uniform(key_list[0], (3, QUERIES), jnp.float32) ** block_levels(key_list[0], (3, QUERIES), ((1, 8),), -0.2, 0.2), 0.0, 1.0),
        "cotangent": gaussian(key_list[1], (CH, QUERIES), 1.0, 6.0, ((1, 8),)),
        "slab_ids": with_ends(jax.random.randint(key_list[2], (KN, QUERIES), -1, N_GA), jax.random.fold_in(key_list[2], 1), -1, N_GA - 1).astype(jnp.int32),
        "rel_cells": with_ends(jax.random.randint(key_list[3], (KN, QUERIES), 0, WIN), jax.random.fold_in(key_list[3], 1), 0, WIN - 1).astype(jnp.int32),
        "offsets": with_ends(jax.random.randint(key_list[4], (N_GA, TILES), 0, SLAB_CELLS - WIN + 1), jax.random.fold_in(key_list[4], 1), 0, SLAB_CELLS - WIN).astype(jnp.int32),
        "latent": gaussian(key_list[5], (N_GA, CH, SLAB_CELLS), 1.0, 6.0, ((0, 4), (2, 8))),
        "w_in": gaussian(key_list[6], (HID, 6), 6 ** -0.5, 2.5, (), jnp.float32),
        "b_in": gaussian(key_list[7], (HID,), 0.5, 3.0, (), jnp.float32),
        "w_out": gaussian(key_list[8], (CH, HID), HID ** -0.5, 0.625),
        "b_out": gaussian(key_list[9], (CH,), 0.5, 3.0, (), jnp.float32),
    }


def gelu_exact(values):
    return jax.nn.gelu(values, approximate=False)

def cell_centres(cell, slab):
    along_x = cell // (GX * ZS)
    along_y = cell // ZS % GX
    along_z = cell % ZS + slab * ZS
    return jnp.stack([(along_x.astype(jnp.float32) + 0.5) / GX, (along_y.astype(jnp.float32) + 0.5) / GX, (along_z.astype(jnp.float32) + 0.5) / GX], 0)

def reference(query_points, cotangent, slab_ids, rel_cells, offsets, latent, w_in, b_in, w_out, b_out):
    cells_slab = GX * GX * ZS
    latent_flat = jnp.transpose(latent, (1, 0, 2)).reshape(CH, N_GA * cells_slab)
    per_block = TILE * math.gcd(TILES, 64)
    count = QUERIES // per_block

    def reshape_blocks(values):
        return values.reshape(values.shape[0], count, per_block).transpose(1, 0, 2)

    def advance(running, inputs_block):
        grid_sum, totals = running
        number, points, cot_cols, slabs, rels = inputs_block
        tile_ids = (number * per_block + jnp.arange(per_block, dtype=jnp.int32)) // TILE
        slab_safe = jnp.maximum(slabs, 0)
        cell = offsets[slab_safe, tile_ids[None, :]] + rels
        flat_index = (slab_safe * cells_slab + cell).reshape(-1).astype(jnp.int32)
        mask_flat = (slabs >= 0).reshape(-1).astype(jnp.float32)
        centres = cell_centres(cell.reshape(-1), slab_safe.reshape(-1))
        features_in = jnp.concatenate([jnp.tile(points, (1, KN)), centres], 0)
        cot_flat = jnp.tile(cot_cols.astype(jnp.float32), (1, KN))
        feats = jnp.take(latent_flat, flat_index, axis=1).astype(jnp.float32)
        preact = jnp.dot(w_in, features_in, precision=lax.Precision.HIGHEST, preferred_element_type=jnp.float32) + b_in[:, None]
        hidden = gelu_exact(preact).astype(jnp.bfloat16)
        kernel = jnp.dot(w_out, hidden, preferred_element_type=jnp.float32) + b_out[:, None]
        grad_cell = (kernel * cot_flat * mask_flat).astype(jnp.bfloat16)
        grad_kernel = (feats * cot_flat * mask_flat).astype(jnp.bfloat16)
        grid_sum = grid_sum.at[:, flat_index].add(grad_cell.astype(jnp.float32))
        grad_w_out = lax.dot_general(grad_kernel, hidden, (((1,), (1,)), ((), ())), preferred_element_type=jnp.float32)
        grad_b_out = lax.optimization_barrier(jnp.sum(grad_kernel.astype(jnp.float32), 1))
        grad_hidden = lax.dot_general(w_out, grad_kernel, (((0,), (0,)), ((), ())), preferred_element_type=jnp.float32)
        grad_pre = jax.vjp(gelu_exact, preact)[1](grad_hidden)[0]
        grad_w_in = lax.dot_general(grad_pre, features_in, (((1,), (1,)), ((), ())), precision=lax.Precision.HIGHEST, preferred_element_type=jnp.float32)
        grad_b_in = lax.optimization_barrier(jnp.sum(grad_pre, 1))
        parts = (grad_w_in, grad_b_in, grad_w_out, grad_b_out)
        totals = tuple((old + new for old, new in zip(totals, parts)))
        return ((grid_sum, totals), None)
    start_totals = (jnp.zeros((HID, 6), jnp.float32), jnp.zeros((HID,), jnp.float32), jnp.zeros((CH, HID), jnp.float32), jnp.zeros((CH,), jnp.float32))
    start_grid = jnp.zeros((CH, N_GA * cells_slab), jnp.float32)
    inputs_all = (jnp.arange(count, dtype=jnp.int32), reshape_blocks(query_points), reshape_blocks(cotangent), reshape_blocks(slab_ids), reshape_blocks(rel_cells))
    (grid_sum, totals), _ = lax.scan(advance, (start_grid, start_totals), inputs_all)
    scale = float(QUERIES) ** (-0.5)
    grid_grad = grid_sum.reshape(CH, N_GA, cells_slab).transpose(1, 0, 2)
    return (grid_grad, totals[0] * scale, totals[1] * scale, totals[2] * scale, totals[3] * scale)
```

```python
import functools
import math

import jax
import jax.numpy as jnp
from jax import lax
from jax.experimental import pallas as pl
from jax.experimental.pallas import tpu as pltpu
from jax.sharding import PartitionSpec as P


TILE = 128
WIN = 512
GX = 64
ZS = 4
LANES = 128
CHUNK = 256
REACH = WIN + LANES
LANE_BIT = 9
SHIFT_BIT = 16
LIVE = 1 << 24
HALF_ROOT = 0.7071067811865476
DENSITY = 0.3989422804014327


def compact_kernel(slots, slab_ref, slabs_ref, rels_ref, out_ref):
    tiles = slabs_ref.shape[1] // TILE
    here = slab_ref[0]
    slabs = jnp.concatenate([slabs_ref[:, t * TILE:(t + 1) * TILE] for t in range(tiles)], 0)
    rels = jnp.concatenate([rels_ref[:, t * TILE:(t + 1) * TILE] for t in range(tiles)], 0)
    rows = tiles * slots
    live = slabs == here
    lane = lax.broadcasted_iota(jnp.int32, (rows, TILE), 1)
    upper = (
        lax.broadcasted_iota(jnp.int32, (TILE, TILE), 0)
        <= lax.broadcasted_iota(jnp.int32, (TILE, TILE), 1)
    ).astype(jnp.float32).astype(jnp.bfloat16)
    flags = live.astype(jnp.float32).astype(jnp.bfloat16)
    prefix = jnp.dot(flags, upper, preferred_element_type=jnp.float32)
    every = jnp.ones((TILE, TILE), jnp.bfloat16)
    totals = jnp.dot(flags, every, preferred_element_type=jnp.float32)
    row_a = lax.broadcasted_iota(jnp.int32, (rows, rows), 0)
    row_b = lax.broadcasted_iota(jnp.int32, (rows, rows), 1)
    before = ((row_a // slots == row_b // slots) & (row_b < row_a)).astype(jnp.float32).astype(jnp.bfloat16)
    starts = jnp.dot(before, totals.astype(jnp.bfloat16), preferred_element_type=jnp.float32)
    starts = starts.astype(jnp.int32)
    totals = totals.astype(jnp.int32)
    move_by = lane - prefix.astype(jnp.int32) + 1
    held = jnp.where(live, rels + lane * (1 << LANE_BIT) + move_by * (1 << SHIFT_BIT) + LIVE, 0)
    for bit in range(7):
        step = 1 << bit
        flag = 1 << (SHIFT_BIT + bit)
        come = pltpu.roll(held, TILE - step, 1)
        held = jnp.where(come & flag != 0, come, jnp.where(held & flag != 0, 0, held))
    for t in range(tiles):
        part = held[t * slots:(t + 1) * slots]
        start = starts[t * slots:(t + 1) * slots]
        total = totals[t * slots:(t + 1) * slots]
        spots = lax.broadcasted_iota(jnp.int32, (slots, TILE), 1)
        lines = []
        for r in range(slots):
            local = spots + r * TILE - start
            own = (local >= 0) & (local < total)
            got = jnp.take_along_axis(part, jnp.clip(local, 0, TILE - 1), axis=1)
            lines.append(jnp.sum(jnp.where(own, got, 0), axis=0, keepdims=True))
        out_ref[t] = jnp.concatenate(lines, 0)


def erf_of(x):
    return lax.erf(x)


def entry_values(chunk, slab, anchor, base, meta, points, cot, win_ref):
    lines = [meta[pl.ds(chunk * 2 + half, 1), :] for half in range(2)]
    packed = jnp.concatenate(lines, 1)
    rel = packed & (WIN - 1)
    picks = [(line >> LANE_BIT) & (TILE - 1) for line in lines]
    valid = packed >= LIVE
    cell = rel + anchor
    spot = jnp.where(valid, cell - base, -1)
    coords = jnp.concatenate(
        [jnp.take_along_axis(points, jnp.broadcast_to(p, points.shape), axis=1) for p in picks], 1
    )
    cots = jnp.concatenate(
        [jnp.take_along_axis(cot, jnp.broadcast_to(p, cot.shape), axis=1) for p in picks], 1
    )
    along_x = ((cell >> 8).astype(jnp.float32) + 0.5) / GX
    along_y = (((cell >> 2) & (GX - 1)).astype(jnp.float32) + 0.5) / GX
    along_z = (((cell & (ZS - 1)) + slab * ZS).astype(jnp.float32) + 0.5) / GX
    inputs = [coords[0:1], coords[1:2], coords[2:3], along_x, along_y, along_z]
    preact = jnp.concatenate([win_ref[6]] * 2, 1)
    for number, line in enumerate(inputs):
        preact = preact + jnp.concatenate([win_ref[number]] * 2, 1) * line
    hot = lax.broadcasted_iota(jnp.int32, (REACH, CHUNK), 0) == spot
    hot = hot.astype(jnp.float32).astype(jnp.bfloat16)
    return preact, inputs, cots, hot


def tile_place(offsets_ref, tile, cells):
    anchor = offsets_ref[tile]
    base = jnp.minimum(anchor // LANES * LANES, cells - REACH)
    return anchor, pl.multiple_of(base, LANES)


def mask_of(place, bits):
    mask = 0
    for number, bit in enumerate(reversed(bits)):
        if place >> number & 1:
            mask |= bit
    return mask


def scatter_kernel(group, orders, offsets_ref, chunks_ref, slab_ref, meta_ref, points_ref, cot_ref,
                   win_ref, wout_ref, bout_ref, *refs):
    out_refs, grid_ref = refs[:-1], refs[-1]
    step = pl.program_id(0)
    cells = grid_ref.shape[1]
    slab = slab_ref[0]

    @pl.when(step == 0)
    def _():
        grid_ref[...] = jnp.zeros_like(grid_ref)

    most = chunks_ref[step * group]
    for g in range(1, group):
        most = jnp.maximum(most, chunks_ref[step * group + g])

    def body(chunk, carry):
        updates = []
        for g in range(group):
            anchor, base = tile_place(offsets_ref, step * group + g, cells)
            columns = slice(g * TILE, (g + 1) * TILE)
            cot = cot_ref[:, columns].astype(jnp.float32)
            preact, _, cots, hot = entry_values(
                chunk, slab, anchor, base, meta_ref.at[g], points_ref[:, columns], cot, win_ref)
            hidden = (0.5 * preact * (1.0 + erf_of(preact * HALF_ROOT))).astype(jnp.bfloat16)
            kernel = jnp.dot(wout_ref[...], hidden, preferred_element_type=jnp.float32)
            kernel = kernel + jnp.concatenate([bout_ref[...]] * 2, 1)
            grad_cell = (kernel * cots).astype(jnp.bfloat16)
            updates.append((base, lax.dot_general(
                grad_cell, hot, (((1,), (1,)), ((), ())), preferred_element_type=jnp.float32)))
        for base, update in updates:
            grid_ref[:, pl.ds(base, REACH)] += update
        return carry

    lax.fori_loop(0, most, body, 0)

    @pl.when(step == pl.num_programs(0) - 1)
    def _():
        half, own = out_refs[0].shape[1:]
        for number, (out_ref, bits) in enumerate(zip(out_refs, orders)):
            for place in range(out_ref.shape[0]):
                owner = slab_ref[1] ^ mask_of(place, bits)
                columns = pl.ds(pl.multiple_of(owner * own, own), own)
                out_ref[place] = grid_ref[pl.ds(number * half, half), columns].astype(out_ref.dtype)


def weight_kernel(group, offsets_ref, chunks_ref, slab_ref, meta_ref, points_ref, cot_ref,
                  win_ref, wout_t_ref, latent_ref, out_ref, slab_feats, total_ref):
    step = pl.program_id(0)
    cells = slab_feats.shape[1]
    slab = slab_ref[0]
    channels = cot_ref.shape[0]
    units = wout_t_ref.shape[0]

    @pl.when(step == 0)
    def _():
        total_ref[...] = jnp.zeros_like(total_ref)
        own = latent_ref.shape[2]
        for owner in range(latent_ref.shape[0]):
            slab_feats[:, owner * own:(owner + 1) * own] = latent_ref[owner]

    most = chunks_ref[step * group]
    for g in range(1, group):
        most = jnp.maximum(most, chunks_ref[step * group + g])

    def body(chunk, carry):
        total = None
        for g in range(group):
            anchor, base = tile_place(offsets_ref, step * group + g, cells)
            columns = slice(g * TILE, (g + 1) * TILE)
            cot = cot_ref[:, columns].astype(jnp.float32)
            preact, inputs, cots, hot = entry_values(
                chunk, slab, anchor, base, meta_ref.at[g], points_ref[:, columns], cot, win_ref)
            window = slab_feats[:, pl.ds(base, REACH)]
            feats = jnp.dot(window, hot, preferred_element_type=jnp.float32)
            grad_kernel = (feats * cots).astype(jnp.bfloat16)
            cdf = 0.5 * (1.0 + erf_of(preact * HALF_ROOT))
            hidden = (preact * cdf).astype(jnp.bfloat16)
            slope = cdf + preact * (DENSITY * jnp.exp(-0.5 * preact * preact))
            grad_hidden = jnp.dot(wout_t_ref[...], grad_kernel, preferred_element_type=jnp.float32)
            grad_pre = grad_hidden * slope
            pre_hi = grad_pre.astype(jnp.bfloat16)
            pre_lo = (grad_pre - pre_hi.astype(jnp.float32)).astype(jnp.bfloat16)
            ones = jnp.ones((1, CHUNK), jnp.float32)
            lines = jnp.concatenate(inputs + [ones, ones * 0.0], 0)
            in_hi = lines.astype(jnp.bfloat16).astype(jnp.float32)
            both = jnp.concatenate([in_hi, lines - in_hi], 0).astype(jnp.bfloat16)
            left = jnp.concatenate([grad_kernel, pre_hi, pre_lo], 0)
            right = jnp.concatenate([hidden, both], 0)
            update = lax.dot_general(
                left, right, (((1,), (1,)), ((), ())), preferred_element_type=jnp.float32)
            total = update if total is None else total + update
        total_ref[...] += total
        return carry

    lax.fori_loop(0, most, body, 0)

    @pl.when(step == pl.num_programs(0) - 1)
    def _():
        out_ref[0:channels] = total_ref[0:channels]
        out_ref[channels:channels + units] = (
            total_ref[channels:channels + units] + total_ref[channels + units:channels + 2 * units])


def exchange(values, axis, bit):
    size = lax.axis_size(axis)
    return lax.ppermute(values, axis, [(i, i ^ bit) for i in range(size)])


def butterfly(values, axis):
    size = lax.axis_size(axis)
    if size & (size - 1):
        return lax.psum(values, axis)
    bit = 1
    while bit < size:
        values = values + exchange(values, axis, bit)
        bit *= 2
    return values


def halve(values, bits):
    for number, bit in enumerate(bits):
        middle = values.shape[0] // 2
        come = exchange(values[middle:], "pb", bit)
        values = values[:middle].astype(jnp.float32) + come.astype(jnp.float32)
        if number < len(bits) - 1:
            values = values.astype(jnp.bfloat16)
    return values[0]


def parts(query_points, cotangent, slab_ids, rel_cells, offsets, latent, w_in, b_in, w_out, b_out):
    channels, own_cells = latent.shape[1:]
    owners = lax.axis_size("pb")
    slots, queries_dev = slab_ids.shape
    units = w_in.shape[0]
    tiles = queries_dev // TILE
    group = math.gcd(tiles, 2)
    cells = owners * own_cells
    slab = jnp.stack([lax.axis_index("ga"), lax.axis_index("pb")]).astype(jnp.int32)
    bits = [1 << number for number in range(owners.bit_length() - 1)]
    assert owners == 1 << len(bits)
    orders = [bits, bits[:1] + bits[:0:-1]]

    gathered = lax.all_gather(latent[0], "pb", axis=0)

    counts = jnp.sum((slab_ids == slab[0]).astype(jnp.int32).reshape(slots, tiles, TILE), (0, 2))
    chunks = (counts + CHUNK - 1) // CHUNK
    anchors = offsets[0]
    smem = pl.BlockSpec(memory_space=pltpu.SMEM)
    vmem = pl.BlockSpec(memory_space=pltpu.VMEM)
    meta = pl.pallas_call(
        functools.partial(compact_kernel, slots),
        out_shape=jax.ShapeDtypeStruct((tiles, slots, TILE), jnp.int32),
        in_specs=[smem, vmem, vmem],
        out_specs=vmem,
        name="compact",
        cost_estimate=pl.CostEstimate(flops=10**8, bytes_accessed=queries_dev * slots * 12, transcendentals=0),
    )(slab, slab_ids, rel_cells)

    points = jnp.pad(query_points, ((0, 5), (0, 0)))
    w_lines = jnp.concatenate([w_in.T, b_in[None]], 0)
    w_lines = jnp.broadcast_to(w_lines[:, :, None], (7, units, LANES))
    b_lines = jnp.broadcast_to(b_out[:, None], (channels, LANES))

    def whole(shape):
        return pl.BlockSpec(shape, lambda i, *_: (0,) * len(shape))

    def by_tile(rows):
        return pl.BlockSpec((rows, group * TILE), lambda i, *_: (0, i))

    meta_spec = pl.BlockSpec((group, slots, TILE), lambda i, *_: (i, 0, 0))
    shared = [meta_spec, by_tile(8), by_tile(channels), whole(w_lines.shape)]
    work = 4 * channels * REACH * tiles * CHUNK * 4
    params = pltpu.CompilerParams(
        dimension_semantics=("arbitrary",), vmem_limit_bytes=40 * 1024 * 1024)
    scatter_call = pl.pallas_call(
        functools.partial(scatter_kernel, group, orders),
        out_shape=[jax.ShapeDtypeStruct((owners, channels // 2, own_cells), jnp.bfloat16)] * 2,
        grid_spec=pltpu.PrefetchScalarGridSpec(
            num_scalar_prefetch=3,
            grid=(tiles // group,),
            in_specs=shared + [whole(w_out.shape), whole(b_lines.shape)],
            out_specs=[whole((owners, channels // 2, own_cells))] * 2,
            scratch_shapes=[pltpu.VMEM((channels, cells), jnp.float32)],
        ),
        compiler_params=params,
        name="scatter",
        cost_estimate=pl.CostEstimate(flops=work, bytes_accessed=10**7, transcendentals=0),
    )
    partial_grad = scatter_call(
        anchors, chunks, slab, meta, points, cotangent, w_lines, w_out, b_lines)

    owned = jnp.concatenate([halve(p, o) for p, o in zip(partial_grad, orders)], 0)

    weights_call = pl.pallas_call(
        functools.partial(weight_kernel, group),
        out_shape=jax.ShapeDtypeStruct((channels + units, units + 16), jnp.float32),
        grid_spec=pltpu.PrefetchScalarGridSpec(
            num_scalar_prefetch=3,
            grid=(tiles // group,),
            in_specs=shared + [whole((units, channels)), whole(gathered.shape)],
            out_specs=whole((channels + units, units + 16)),
            scratch_shapes=[
                pltpu.VMEM((channels, cells), jnp.bfloat16),
                pltpu.VMEM((channels + 2 * units, units + 16), jnp.float32),
            ],
        ),
        compiler_params=params,
        name="weights",
        cost_estimate=pl.CostEstimate(flops=work, bytes_accessed=10**7, transcendentals=0),
    )
    sums = weights_call(
        anchors, chunks, slab, meta, points, cotangent, w_lines, w_out.T, gathered)

    scale = float(queries_dev * owners) ** (-0.5)
    sums = butterfly(butterfly(sums, "pb"), "ga") * scale
    ins = sums[channels:, units:units + 8] + sums[channels:, units + 8:units + 16]
    return (
        owned.astype(jnp.float32)[None],
        ins[:, :6],
        ins[:, 6],
        sums[:channels, :units],
        sums[:channels, units + 6],
    )


def solution(mesh):
    return jax.shard_map(
        parts,
        mesh=mesh,
        in_specs=(
            P(None, "pb"),
            P(None, "pb"),
            P(None, "pb"),
            P(None, "pb"),
            P("ga", "pb"),
            P("ga", None, "pb"),
            P(),
            P(),
            P(),
            P(),
        ),
        out_specs=(P("ga", None, "pb"), P(), P(), P(), P()),
        check_vma=False,
    )
```
